32 devices in a mesh: sec: 2 (over y), grp: 4 (over x, core), seq: 4 (over z).
Axes of the slice: x: 2, y: 2, z: 4, core: 2. Of those that a mesh axis runs over, the one named last changes fastest.
Arguments:
- tokens: bfloat16 [8192, 1024], P(('sec', 'grp', 'seq')), may hold values from -6 to 6
- expert_ids: int32 [8192, 1], P(('sec', 'grp', 'seq')), may hold values from 0 to 31; in each aligned block of 256 rows (0 to 255, 256 to 511, ...) at most 16 rows name the same one
- attn_in: bfloat16 [1024, 3072], replicated
- attn_out: bfloat16 [1024, 1024], replicated, may hold values from -0.1875 to 0.1875
- gain_attn: float32 [1024], replicated, may hold values from 0.5 to 1.5
- gain_expert: float32 [1024], replicated, may hold values from 0.5 to 1.5
- router: bfloat16 [1024, 32], replicated, may hold values from -0.1875 to 0.1875
- expert_in: bfloat16 [32, 1024, 2816], P(('sec', 'grp', 'seq')), may hold values from -0.1875 to 0.1875
- expert_out: bfloat16 [32, 2816, 1024], P(('sec', 'grp', 'seq')), may hold values from -0.109375 to 0.109375
Outputs:
- layer_out: bfloat16 [8192, 1024], P(('sec', 'grp', 'seq'))
The draws below stay inside these ranges and needn't reach their ends.
Inputs may be any that keep to these rules, and one draw needn't show every extreme that they name: `expert_ids`: of the 256 tokens of one device at most 16 choose one expert, and on every device some expert is chosen by exactly 16 of them.
All inputs are finite; a program needn't handle non-finite values.
Results may differ from the reference program's by a relative error of at most 0.004.
Values may be sent and summed in bfloat16 or wider, within the bound.
A program may use at most 192 MiB of HBM per device.

```python
import math
import jax
import jax.numpy as jnp
import numpy as np
from jax import lax

D = 1024
HEADS = 16
FF = 2816
TOK_DEV = 256
HEAD_DIM = 64
EXPERTS = 32
MOST = 16
LENGTH = 1024
TOKENS = 8192


def draw_attn_in(key, part):
    values = jax.random.normal(key, (D, 3 * D), jnp.float32) * D ** (-0.5)
    return values.astype(jnp.bfloat16)


def block_scale(key, extent, shards, smallest, largest):
    level = 1.0
    for dim, shards_of in shards:
        heights = jax.random.uniform(jax.random.fold_in(jax.random.fold_in(key, 6), dim), (shards_of,), jnp.float32, smallest / len(shards), largest / len(shards))
        level = level * jnp.repeat(jnp.exp(heights), extent[dim] // shards_of).reshape((-1,) + (1,) * (len(extent) - 1 - dim))
    return level


def deal_out(rng, own, number, rows, number_of, top, reach, slope):
    sequence = jax.random.permutation(rng, number_of)
    packed, usual = shares(number_of, rows * top, reach, slope, True), shares(number_of, rows * top, reach, slope, False)
    places = jnp.arange(number_of)

    def named(sizes, offset_by):
        used = int((sizes > 0).sum())
        fixed = max(1, used // 4)
        shifted = fixed + (places - fixed + offset_by * (used - fixed)) % max(1, number_of - fixed)
        return jnp.zeros((number_of,), jnp.int32).at[sequence[jnp.where(places < fixed, places, shifted)]].set(jnp.asarray(sizes, jnp.int32))

    sizes = jnp.where(number % 4 == 0, named(packed, number // 4), named(usual, number - number // 4 - 1))
    mixed = jax.random.permutation(jax.random.fold_in(own, 3), number_of)
    source_of, taker = mixed[0:number_of // 2 * 2:2], mixed[1:number_of // 2 * 2:2]
    margin = jnp.minimum(sizes[source_of] - 1, reach - sizes[taker]) // 2
    margin = jnp.where((source_of == sequence[0]) | (taker == sequence[0]) | (sizes[taker] == 0), 0, jnp.maximum(margin, 0))
    shifted = jax.random.randint(jax.random.fold_in(own, 4), (number_of // 2,), 0, 1 << 20) % (margin + 1)
    sizes = sizes.at[source_of].add(-shifted).at[taker].add(shifted)
    labels = jnp.searchsorted(jnp.cumsum(sizes), jnp.arange(rows * top), side="right").astype(jnp.int32)
    listing = labels.reshape(top, rows).T
    listing = listing[jax.random.permutation(jax.random.fold_in(own, 1), rows)]
    offset_by = jax.random.randint(jax.random.fold_in(own, 2), (rows, 1), 0, top)
    return jnp.take_along_axis(listing, (jnp.arange(top)[None, :] + offset_by) % top, axis=1)


def shares(amount, total, limit, lean, full):
    portions = [(1 << 20) // math.isqrt(rank ** lean) + 1 for rank in range(1, amount + 1)]
    largest = limit if full else min(limit, max(-(-total // amount), total * portions[0] // sum(portions)))
    least = 1 if total - largest >= amount - 1 else 0
    given, spare = [largest] + [least] * (amount - 1), total - largest - least * (amount - 1)
    while spare > 0:
        movable = [i for i in range(1, amount) if given[i] < largest] or [i for i in range(1, amount) if given[i] < limit]
        whole, remaining = sum([portions[i] for i in movable]), spare
        for i in movable:
            addition = min(limit - given[i], max(1, remaining * portions[i] // whole), spare)
            given[i] = given[i] + addition
            spare = spare - addition
    return np.array(given)


def centred(key, extent, deviation, bound, shards=(), kind=jnp.bfloat16):
    result = deviation * jax.random.normal(key, extent, jnp.float32)
    if shards:
        result = result * block_scale(key, extent, shards, -0.22, 0.18)
    return jnp.clip(result, -bound, bound).astype(kind)


def setup_inputs(seed: int = 0) -> dict:
    splits = jax.random.split(jax.random.key(seed), 10)
    tokens = centred(splits[0], (TOKENS, D), 1.0, 6.0, ((0, 32),))
    expert_ids_keys = jax.random.split(jax.random.fold_in(splits[1], 1), TOKENS // TOK_DEV)
    expert_ids_turns = jax.random.permutation(jax.random.fold_in(splits[1], 3), TOKENS // TOK_DEV)
    expert_ids = jax.vmap(lambda own, number: deal_out(jax.random.fold_in(splits[1], 2), own, number, TOK_DEV, EXPERTS, 1, MOST, 1))(expert_ids_keys, expert_ids_turns).reshape((TOKENS, 1))
    attn_in = draw_attn_in(jax.random.fold_in(splits[9], 71), 0)
    attn_out = centred(splits[3], (D, D), D ** -0.5, 0.1875)
    gain_attn = jnp.clip(1.0 + 0.1 * jax.random.normal(splits[4], (D,), jnp.float32), 0.5, 1.5)
    gain_expert = jnp.clip(1.0 + 0.1 * jax.random.normal(splits[5], (D,), jnp.float32), 0.5, 1.5)
    router = centred(splits[6], (D, EXPERTS), D ** -0.5, 0.1875)
    expert_in = centred(splits[7], (EXPERTS, D, FF), D ** -0.5, 0.1875, ((0, 32),))
    expert_out = centred(splits[8], (EXPERTS, FF, D), FF ** -0.5, 0.109375, ((0, 32),))
    return dict(tokens=tokens, expert_ids=expert_ids, attn_in=attn_in, attn_out=attn_out, gain_attn=gain_attn, gain_expert=gain_expert, router=router, expert_in=expert_in, expert_out=expert_out)


def normalize(values, gain):
    return values * lax.rsqrt(lax.optimization_barrier(jnp.mean(values * values, -1, keepdims=True)) + 1e-06) * gain.astype(jnp.float32)

def head_attention(query, keys, values):
    scores = jnp.dot(query, keys.T, preferred_element_type=jnp.float32) * query.shape[1] ** (-0.5)
    weights = jax.nn.softmax(scores, -1).astype(jnp.bfloat16)
    return jnp.dot(weights, values, preferred_element_type=jnp.float32).astype(jnp.bfloat16)

def reference(tokens, expert_ids, attn_in, attn_out, gain_attn, gain_expert, router, expert_in, expert_out):
    tokens_f32 = tokens.astype(jnp.float32)
    normed = normalize(tokens_f32, gain_attn).astype(jnp.bfloat16)
    projected = jnp.dot(normed, attn_in, preferred_element_type=jnp.float32).astype(jnp.bfloat16)
    seq_count = TOKENS // LENGTH
    head_parts = projected.reshape(seq_count, LENGTH, 3, HEADS, HEAD_DIM).transpose(0, 3, 2, 1, 4)
    head_parts = head_parts.reshape(seq_count * HEADS, 3, LENGTH, HEAD_DIM)
    context = lax.map(lambda head_item: head_attention(head_item[0], head_item[1], head_item[2]), head_parts)
    context = context.reshape(seq_count, HEADS, LENGTH, HEAD_DIM).transpose(0, 2, 1, 3).reshape(TOKENS, D)
    hidden = tokens_f32 + jnp.dot(context, attn_out, preferred_element_type=jnp.float32)
    normed2 = normalize(hidden, gain_expert).astype(jnp.bfloat16)
    picked = expert_ids[:, 0]
    logits = jnp.dot(normed2, router, preferred_element_type=jnp.float32)
    gate_value = jax.nn.sigmoid(jnp.take_along_axis(logits, expert_ids, 1)[:, 0])
    capacity = TOKENS // TOK_DEV * MOST
    padded_rows = jnp.concatenate([normed2, jnp.zeros((1, D), jnp.bfloat16)], 0)

    def one_expert(expert_index):
        slot_rows = jnp.nonzero(picked == expert_index, size=capacity, fill_value=TOKENS)[0].astype(jnp.int32)
        inputs = padded_rows[slot_rows]
        inner_act = jax.nn.relu(jnp.dot(inputs, expert_in[expert_index], preferred_element_type=jnp.float32)).astype(jnp.bfloat16)
        return (slot_rows, jnp.dot(inner_act, expert_out[expert_index], preferred_element_type=jnp.float32).astype(jnp.bfloat16))
    slot_rows, outputs = lax.map(one_expert, jnp.arange(EXPERTS, dtype=jnp.int32))
    combined = jnp.zeros((TOKENS + 1, D), jnp.float32).at[slot_rows.reshape(-1)].add(outputs.reshape(-1, D).astype(jnp.float32))
    combined = combined[:TOKENS]
    return (hidden + gate_value[:, None] * combined).astype(jnp.bfloat16)
```

```python
import functools

import jax
import jax.numpy as jnp
from jax import lax
from jax.experimental import pallas as pl
from jax.experimental.pallas import tpu as pltpu
from jax.sharding import PartitionSpec as P

HEADS = 16
AXES = ("sec", "grp", "seq")
MESH = pl.DeviceIdType.MESH
VMEM_LIMIT = 60 * 1024 * 1024


def normalize(values, gain):
    return values * lax.rsqrt(jnp.mean(values * values, -1, keepdims=True) + 1e-06) * gain


def layer_kernel(
    sizes,
    head_dim,
    tok_ref,
    ids_row_ref,
    win_hbm,
    wout_hbm,
    gain_ref,
    gain2_ref,
    router_ref,
    w1_hbm,
    w2_hbm,
    out_ref,
    shards,
    slot_rows,
    win,
    wout,
    query,
    kv,
    acc,
    peak,
    hidden,
    rows_buf,
    arrived,
    result,
    back,
    final_in,
    inner,
    w1,
    w_sem,
    right_sem,
    left_sem,
    recv_sem,
    slot_send,
    slot_recv,
    out_sem,
    in_sem,
    reply_sem,
    back_sem,
    home_send,
    home_recv,
):
    secs, grps, ranks = sizes
    groups = secs * grps
    experts = groups * ranks
    final_out = query
    context = inner.at[:, 0 : tok_ref.shape[1]]
    most = rows_buf.shape[2]
    slots = groups * most
    rows, width = tok_ref.shape
    pair = 2 * head_dim
    pairs = width // pair
    piece = rows // 2
    me = lax.axis_index("seq")
    load_in = pltpu.make_async_copy(win_hbm, win, w_sem.at[0])
    load_out = pltpu.make_async_copy(wout_hbm, wout, w_sem.at[1])
    load1 = pltpu.make_async_copy(w1_hbm, w1, w_sem.at[2])
    load_in.start()
    load_out.start()
    load1.start()
    sec, grp = lax.axis_index("sec"), lax.axis_index("grp")
    group = sec * grps + grp
    has_left, has_right = me > 0, me < ranks - 1
    short = jnp.minimum(me, ranks - 1 - me)
    longest = ranks - 1 - short
    barrier = pltpu.get_barrier_semaphore()

    def place(other_group, other_rank):
        return (other_group // grps, other_group % grps, other_rank)

    def greet_column(offset, carry):
        pl.semaphore_signal(
            barrier, inc=1, device_id=place(group, (me + offset) % ranks), device_id_type=MESH
        )
        return carry

    def greet_plane(offset, carry):
        pl.semaphore_signal(
            barrier, inc=1, device_id=place((group + offset) % groups, me), device_id_type=MESH
        )
        return carry

    lax.fori_loop(1, ranks, greet_column, 0)
    lax.fori_loop(1, groups, greet_plane, 0)
    pl.semaphore_wait(barrier, ranks + groups - 2)

    def carry_to(other, sems, source, index, part):
        return pltpu.make_async_remote_copy(
            src_ref=source,
            dst_ref=shards.at[index, part],
            send_sem=sems.at[index, part],
            recv_sem=recv_sem.at[index, part],
            device_id={"seq": other},
            device_id_type=MESH,
        )

    def to_right(source, index, part):
        return carry_to(me + 1, right_sem, source, index, part)

    def to_left(source, index, part):
        return carry_to(me - 1, left_sem, source, index, part)

    for part in range(2):
        half = tok_ref.at[pl.ds(part * piece, piece)]

        @pl.when(has_right)
        def _(half=half, part=part):
            to_right(half, me, part).start()

        @pl.when(has_left)
        def _(half=half, part=part):
            to_left(half, me, part).start()

    bands = [(b, min(width, w2_hbm.shape[0] - b)) for b in range(0, w2_hbm.shape[0], width)]

    def load_band(i):
        begin, size = bands[i]
        return pltpu.make_async_copy(
            w2_hbm.at[pl.ds(begin, size)],
            win.at[pl.ds(0, size), pl.ds(begin, width)],
            w_sem.at[3 + i],
        )

    def order(n):
        step = (n + 1) // 2
        near = jnp.where(n % 2 == 1, me - step, me + step)
        far = jnp.where(2 * me < ranks, me + (n - short), me - (n - short))
        return jnp.where(n <= 2 * short, near, far)

    ids_row = ids_row_ref[...].astype(jnp.float32)
    chosen_row = (
        lax.broadcasted_iota(jnp.int32, (experts, rows), 0).astype(jnp.float32) == ids_row
    ).astype(jnp.float32)
    down = lax.broadcasted_iota(jnp.int32, (rows, rows), 0)
    across = lax.broadcasted_iota(jnp.int32, (rows, rows), 1)
    above = (down < across).astype(jnp.float32).astype(jnp.bfloat16)
    earlier_row = jnp.dot(chosen_row.astype(jnp.bfloat16), above, preferred_element_type=jnp.float32)
    slot_row = ids_row * most + jnp.sum(earlier_row * chosen_row, 0, keepdims=True)
    slot_column = jnp.sum(jnp.where(down == across, slot_row, 0.0), 1, keepdims=True)
    slot_rows[me] = jnp.broadcast_to(slot_row, slot_rows.shape[1:])

    def send_slots(other):
        return pltpu.make_async_remote_copy(
            src_ref=slot_rows.at[me],
            dst_ref=slot_rows.at[me],
            send_sem=slot_send.at[other],
            recv_sem=slot_recv.at[me],
            device_id=place(group, other),
            device_id_type=MESH,
        )

    def receive_slots(other):
        return pltpu.make_async_remote_copy(
            src_ref=slot_rows.at[other],
            dst_ref=slot_rows.at[other],
            send_sem=slot_send.at[other],
            recv_sem=slot_recv.at[other],
            device_id=place(group, other),
            device_id_type=MESH,
        )

    def start_slots(offset, carry):
        send_slots((me + offset) % ranks).start()
        return carry

    lax.fori_loop(1, ranks, start_slots, 0)

    def label(rank, shape, dim):
        column = lax.broadcasted_iota(jnp.int32, shape, dim).astype(jnp.float32)
        block = jnp.floor((column + 0.5) * (1.0 / most))
        return (block * ranks + rank.astype(jnp.float32)) * most + (column - block * most)

    shards[me, 0] = tok_ref[0:piece]
    shards[me, 1] = tok_ref[piece:rows]
    lane = lax.broadcasted_iota(jnp.int32, (slots, pair), 1)
    first = lane < head_dim
    own_label = label(me, (slots, rows), 0)
    col_block = 256 if width % 256 == 0 else width

    def project(pos, index, part):
        normed = normalize(shards[index, part].astype(jnp.float32), gain_ref[...]).astype(jnp.bfloat16)
        for c in range(0, 2 * width, col_block):
            kv[2 * pos + part, :, c : c + col_block] = jnp.dot(
                normed,
                win[:, width + c : width + c + col_block],
                preferred_element_type=jnp.float32,
            ).astype(jnp.bfloat16)

    def queries(pos, index):
        pick = (own_label == slot_rows[index, 0:1]).astype(jnp.float32).astype(jnp.bfloat16)
        chosen = jnp.dot(
            pick, shards[index].reshape(rows, width), preferred_element_type=jnp.float32
        )
        hidden[pos] = chosen
        normed = normalize(chosen, gain_ref[...]).astype(jnp.bfloat16)
        for c in range(0, width, col_block):
            query[pos, :, c : c + col_block] = jnp.dot(
                normed, win[:, c : c + col_block], preferred_element_type=jnp.float32
            ).astype(jnp.bfloat16) * jnp.bfloat16(head_dim ** (-0.5))

    def scores_of(n, p, begin, end):
        keys = kv[begin:end, :, p * pair : (p + 1) * pair].reshape((end - begin) * piece, pair)
        both = query[n, :, p * pair : (p + 1) * pair]
        none = jnp.zeros_like(both)
        heads = jnp.concatenate([jnp.where(first, both, none), jnp.where(first, none, both)], 0)
        return lax.dot_general(
            heads, keys, (((1,), (1,)), ((), ())), preferred_element_type=jnp.float32
        )

    def mix(weights, p, begin, end):
        values = kv[begin:end, :, width + p * pair : width + (p + 1) * pair]
        values = values.reshape((end - begin) * piece, pair)
        return jnp.dot(
            weights,
            jnp.concatenate([values, jnp.ones_like(values)], 1),
            preferred_element_type=jnp.float32,
        )

    known = 2 * (ranks - 1)

    def begin_attention(n):
        for p in range(pairs):
            scores = scores_of(n, p, 0, known)
            new = jnp.max(scores, -1, keepdims=True)
            update = mix(jnp.exp(scores - new).astype(jnp.bfloat16), p, 0, known)
            weight = update[:, pair : 2 * pair]
            acc[n, p] = update[:, 0:pair] / weight
            peak[n, p] = new + jnp.log(weight)

    def put_context(p, value, weight):
        mean = value / weight
        context[:, p * pair : (p + 1) * pair] = jnp.where(
            first, mean[0:slots], mean[slots : 2 * slots]
        ).astype(jnp.bfloat16)

    def end_attention(n):
        for p in range(pairs):
            scores = scores_of(n, p, known, known + 2)
            old = peak[n, p]
            new = jnp.maximum(old, jnp.max(scores, -1, keepdims=True))
            scale = jnp.exp(old - new)
            spread = jnp.concatenate([new] * (rows // pair), 1) if rows % pair == 0 else new[:, 0:1]
            update = mix(jnp.exp(scores - spread).astype(jnp.bfloat16), p, known, known + 2)
            put_context(
                p,
                acc[n, p] * scale + update[:, 0:pair],
                scale + update[:, pair : 2 * pair],
            )

    def whole_attention(n):
        for p in range(pairs):
            scores = scores_of(n, p, 0, known + 2)
            new = jnp.max(scores, -1, keepdims=True)
            update = mix(jnp.exp(scores - new).astype(jnp.bfloat16), p, 0, known + 2)
            put_context(p, update[:, 0:pair], update[:, pair : 2 * pair])

    def over_plane(act):
        def one(offset, carry):
            act((group + offset) % groups)
            return carry

        lax.fori_loop(1, groups, one, 0)

    def send(n, other):
        return pltpu.make_async_remote_copy(
            src_ref=rows_buf.at[n, other],
            dst_ref=arrived.at[n, group],
            send_sem=out_sem.at[n, other],
            recv_sem=in_sem.at[n, group],
            device_id=place(other, me),
            device_id_type=MESH,
        )

    def receive(n, other):
        return pltpu.make_async_remote_copy(
            src_ref=rows_buf.at[n, other],
            dst_ref=arrived.at[n, other],
            send_sem=out_sem.at[n, other],
            recv_sem=in_sem.at[n, other],
            device_id=place(other, me),
            device_id_type=MESH,
        )

    def reply(n, other):
        return pltpu.make_async_remote_copy(
            src_ref=result.at[n, other],
            dst_ref=back.at[n, group],
            send_sem=reply_sem.at[n, other],
            recv_sem=back_sem.at[n, group],
            device_id=place(other, me),
            device_id_type=MESH,
        )

    def returned(n, other):
        return pltpu.make_async_remote_copy(
            src_ref=result.at[n, other],
            dst_ref=back.at[n, other],
            send_sem=reply_sem.at[n, other],
            recv_sem=back_sem.at[n, other],
            device_id=place(other, me),
            device_id_type=MESH,
        )

    def send_home(n):
        return pltpu.make_async_remote_copy(
            src_ref=final_out.at[n],
            dst_ref=final_in.at[me],
            send_sem=home_send.at[n],
            recv_sem=home_recv.at[me],
            device_id=place(group, order(n)),
            device_id_type=MESH,
        )

    def receive_home(n):
        return pltpu.make_async_remote_copy(
            src_ref=final_out.at[n],
            dst_ref=final_in.at[order(n)],
            send_sem=home_send.at[n],
            recv_sem=home_recv.at[order(n)],
            device_id=place(group, order(n)),
            device_id_type=MESH,
        )

    def dispatch(n):
        rows_out = hidden[n] + jnp.dot(
            context[...], wout[...], preferred_element_type=jnp.float32
        )
        hidden[n] = rows_out
        rows_buf[n] = (
            normalize(rows_out, gain2_ref[...]).astype(jnp.bfloat16).reshape(groups, most, width)
        )
        over_plane(lambda g: send(n, g).start())
        arrived[n, group] = rows_buf[n, group]

    hidden_units = w1.shape[1]
    block = 256 if hidden_units % 256 == 0 else hidden_units

    def work(n):
        over_plane(lambda g: receive(n, g).wait_recv())
        batch = arrived[n].reshape(slots, width)
        for c in range(0, hidden_units, block):
            inner[:, c : c + block] = jax.nn.relu(
                jnp.dot(batch, w1[:, c : c + block], preferred_element_type=jnp.float32)
            ).astype(jnp.bfloat16)
        for c in range(0, width, col_block):
            result[n, :, :, c : c + col_block] = (
                sum(
                    jnp.dot(
                        inner[:, b : b + size],
                        win[0:size, b + c : b + c + col_block],
                        preferred_element_type=jnp.float32,
                    )
                    for b, size in bands
                )
                .astype(jnp.bfloat16)
                .reshape(groups, most, col_block)
            )
        over_plane(lambda g: reply(n, g).start())
        back[n, group] = result[n, group]

    row_block = jnp.floor(
        (lax.broadcasted_iota(jnp.int32, (slots, experts), 0).astype(jnp.float32) + 0.5) * (1.0 / most)
    )
    own_expert = lax.broadcasted_iota(jnp.int32, (slots, experts), 1).astype(
        jnp.float32
    ) == row_block * ranks + me.astype(jnp.float32)

    def combine(n):
        logits = lax.dot_general(
            rows_buf[n].reshape(slots, width),
            router_ref[...],
            (((1,), (1,)), ((), ())),
            preferred_element_type=jnp.float32,
        )
        gate = jax.nn.sigmoid(jnp.sum(jnp.where(own_expert, logits, 0.0), 1, keepdims=True))
        over_plane(lambda g: returned(n, g).wait_recv())
        final_out[n] = (
            hidden[n] + gate * back[n].reshape(slots, width).astype(jnp.float32)
        ).astype(jnp.bfloat16)

    def combine_far(n):
        combine(n)
        send_home(n).start()

    load_in.wait()
    project(0, me, 0)
    project(0, me, 1)
    queries(0, me)

    def begin(n, carry):
        begin_attention(n)
        return carry

    def step(turn, carry):
        distance, part = 1 + turn // 2, turn % 2
        low, high = me - distance, me + distance

        @pl.when((distance == longest) & (part == 0))
        def _():
            lax.fori_loop(0, ranks - 1, begin, 0)

        @pl.when(low >= 0)
        def _():
            to_left(shards.at[low, part], low, part).wait_recv()

            @pl.when(has_right)
            def _():
                to_right(shards.at[low, part], low, part).start()

        @pl.when(high < ranks)
        def _():
            to_right(shards.at[high, part], high, part).wait_recv()

            @pl.when(has_left)
            def _():
                to_left(shards.at[high, part], high, part).start()

        def side(which, inner_carry):
            index = jnp.where(which == 0, low, high)
            pos = jnp.where(distance <= short, 2 * distance - 1 + which, short + distance)

            @pl.when((index >= 0) & (index < ranks))
            def _():
                project(pos, index, part)

                @pl.when((part == 1) & (distance < longest))
                def _():
                    receive_slots(index).wait_recv()
                    queries(pos, index)

            return inner_carry

        lax.fori_loop(0, 2, side, 0)
        return carry

    lax.fori_loop(0, 2 * (ranks - 1), step, 0)
    load_out.wait()
    end_attention(ranks - 2)
    dispatch(ranks - 2)
    receive_slots(order(ranks - 1)).wait_recv()
    queries(ranks - 1, order(ranks - 1))
    for i in range(len(bands)):
        load_band(i).start()
    whole_attention(ranks - 1)
    dispatch(ranks - 1)

    def rest(turn, carry):
        n = ranks - 3 - turn
        end_attention(n)
        dispatch(n)
        return carry

    lax.fori_loop(0, ranks - 2, rest, 0)
    load1.wait()
    for i in range(len(bands)):
        load_band(i).wait()

    def chunk(turn):
        return jnp.where(turn == 0, ranks - 2, jnp.where(turn == 1, ranks - 1, ranks - 1 - turn))

    def experts_turn(turn, carry):
        work(chunk(turn))

        @pl.when(turn >= 1)
        def _():
            combine_far(chunk(turn - 1))

        return carry

    lax.fori_loop(0, ranks, experts_turn, 0)
    combine(0)
    final_in[me] = final_out[0]

    def arrival(n, carry):
        receive_home(n).wait_recv()
        return carry

    lax.fori_loop(1, ranks, arrival, 0)
    spot = lax.broadcasted_iota(jnp.int32, (rows, ranks * slots), 1).astype(jnp.float32)
    source = jnp.floor((spot + 0.5) * (1.0 / slots))
    spot = spot - source * slots
    target = jnp.floor((spot + 0.5) * (1.0 / most))
    spot = (target * ranks + source) * most + (spot - target * most)
    pick = (spot == slot_column).astype(jnp.float32).astype(jnp.bfloat16)
    for c in range(0, width, col_block):
        out_ref[:, c : c + col_block] = jnp.dot(
            pick,
            final_in[:, :, c : c + col_block].reshape(ranks * slots, col_block),
            preferred_element_type=jnp.float32,
        ).astype(jnp.bfloat16)

    def drain_rank(n, carry):
        over_plane(lambda g: send(n, g).wait_send())
        over_plane(lambda g: reply(n, g).wait_send())
        return carry

    lax.fori_loop(0, ranks, drain_rank, 0)

    def drain_home(n, carry):
        send_home(n).wait_send()
        send_slots((me + n) % ranks).wait_send()
        return carry

    lax.fori_loop(1, ranks, drain_home, 0)

    def drain(index, carry):
        @pl.when(has_right & (index <= me))
        def _():
            for part in range(2):
                to_right(shards.at[index, part], index, part).wait_send()

        @pl.when(has_left & (index >= me))
        def _():
            for part in range(2):
                to_left(shards.at[index, part], index, part).wait_send()

        return carry

    lax.fori_loop(0, ranks, drain, 0)


def layer(tokens, expert_ids, attn_in, attn_out, gain_attn, gain_expert, router, w1, w2):
    rows, width = tokens.shape
    sizes = tuple(lax.axis_size(name) for name in AXES)
    groups, ranks = sizes[0] * sizes[1], sizes[2]
    devices = groups * ranks
    most = max(2, 2 * rows // devices)
    slots = groups * most
    head_dim = width // HEADS
    pair = 2 * head_dim
    pairs = width // pair
    vmem = pl.BlockSpec(memory_space=pltpu.VMEM)
    hbm = pl.BlockSpec(memory_space=pl.ANY)
    blocks = pltpu.VMEM((ranks, groups, most, width), jnp.bfloat16)
    chunks = pltpu.VMEM((ranks, slots, width), jnp.bfloat16)
    running = pltpu.VMEM((ranks - 1, pairs, 2 * slots, pair), jnp.float32)
    per_rank = pltpu.SemaphoreType.DMA((ranks,))
    per_half = pltpu.SemaphoreType.DMA((ranks, 2))
    per_device = pltpu.SemaphoreType.DMA((ranks, groups))
    return pl.pallas_call(
        functools.partial(layer_kernel, sizes, head_dim),
        out_shape=jax.ShapeDtypeStruct((rows, width), jnp.bfloat16),
        in_specs=[vmem, vmem, hbm, hbm, vmem, vmem, vmem, hbm, hbm],
        out_specs=vmem,
        scratch_shapes=[
            pltpu.VMEM((ranks, 2, rows // 2, width), jnp.bfloat16),
            pltpu.VMEM((ranks, 8, rows), jnp.float32),
            pltpu.VMEM(attn_in.shape, jnp.bfloat16),
            pltpu.VMEM(attn_out.shape, jnp.bfloat16),
            chunks,
            pltpu.VMEM((2 * ranks, rows // 2, 2 * width), jnp.bfloat16),
            running,
            running,
            pltpu.VMEM((ranks, slots, width), jnp.float32),
            blocks,
            blocks,
            blocks,
            blocks,
            chunks,
            pltpu.VMEM((slots, w1.shape[1]), jnp.bfloat16),
            pltpu.VMEM(w1.shape, jnp.bfloat16),
            pltpu.SemaphoreType.DMA((3 + -(-w2.shape[0] // width),)),
            per_half,
            per_half,
            per_half,
            per_rank,
            per_rank,
            per_device,
            per_device,
            per_device,
            per_device,
            per_rank,
            per_rank,
        ],
        compiler_params=pltpu.CompilerParams(
            collective_id=0, has_side_effects=True, vmem_limit_bytes=VMEM_LIMIT
        ),
    )(
        tokens,
        expert_ids.reshape(1, rows),
        attn_in,
        attn_out,
        gain_attn[None, :],
        gain_expert[None, :],
        router.T,
        w1,
        w2,
    )


def body(
    tokens, expert_ids, attn_in, attn_out, gain_attn, gain_expert, router, expert_in, expert_out
):
    return layer(
        tokens,
        expert_ids,
        attn_in,
        attn_out,
        gain_attn,
        gain_expert,
        router,
        expert_in[0],
        expert_out[0],
    )


def solution(mesh):
    return jax.shard_map(
        body,
        mesh=mesh,
        in_specs=(P(AXES, None), P(AXES, None), P(), P(), P(), P(), P(), P(AXES, None, None), P(AXES, None, None)),
        out_specs=P(AXES, None),
        check_vma=False,
    )
```

```python
import functools

import jax
import jax.numpy as jnp
from jax import lax
from jax.experimental import pallas as pl
from jax.experimental.pallas import tpu as pltpu
from jax.sharding import PartitionSpec as P

HEADS = 16
AXES = ("sec", "grp", "seq")
MESH = pl.DeviceIdType.MESH
VMEM_LIMIT = 60 * 1024 * 1024


def normalize(values, gain):
    return values * lax.rsqrt(jnp.mean(values * values, -1, keepdims=True) + 1e-06) * gain


def layer_kernel(
    sizes,
    head_dim,
    tok_ref,
    ids_row_ref,
    win_hbm,
    wout_hbm,
    gain_ref,
    gain2_ref,
    router_ref,
    w1_hbm,
    w2_hbm,
    out_ref,
    shards,
    slot_rows,
    win,
    wout,
    query,
    kv,
    acc,
    peak,
    slot_tok,
    hidden,
    gate,
    rows_buf,
    arrived,
    result,
    back,
    inner,
    w1,
    w_sem,
    right_sem,
    left_sem,
    recv_sem,
    slot_send,
    slot_recv,
    out_sem,
    in_sem,
    reply_sem,
    back_sem,
):
    secs, grps, ranks = sizes
    groups = secs * grps
    experts = groups * ranks
    most = rows_buf.shape[2]
    slots = groups * most
    rows, width = tok_ref.shape
    extra = rows // slots
    pair = 2 * head_dim
    pairs = width // pair
    piece = rows // 2
    me = lax.axis_index("seq")
    load_in = pltpu.make_async_copy(win_hbm, win, w_sem.at[0])
    load_out = pltpu.make_async_copy(wout_hbm, wout, w_sem.at[1])
    load1 = pltpu.make_async_copy(w1_hbm, w1, w_sem.at[2])
    load_in.start()
    load_out.start()
    load1.start()
    sec, grp = lax.axis_index("sec"), lax.axis_index("grp")
    group = sec * grps + grp
    has_left, has_right = me > 0, me < ranks - 1
    short = jnp.minimum(me, ranks - 1 - me)
    longest = ranks - 1 - short
    barrier = pltpu.get_barrier_semaphore()

    def place(other_group, other_rank):
        return (other_group // grps, other_group % grps, other_rank)

    def greet_column(offset, carry):
        pl.semaphore_signal(
            barrier, inc=1, device_id=place(group, (me + offset) % ranks), device_id_type=MESH
        )
        return carry

    def greet_plane(offset, carry):
        pl.semaphore_signal(
            barrier, inc=1, device_id=place((group + offset) % groups, me), device_id_type=MESH
        )
        return carry

    lax.fori_loop(1, ranks, greet_column, 0)
    lax.fori_loop(1, groups, greet_plane, 0)
    pl.semaphore_wait(barrier, ranks + groups - 2)

    def carry_to(other, sems, source, index, part):
        return pltpu.make_async_remote_copy(
            src_ref=source,
            dst_ref=shards.at[index, part],
            send_sem=sems.at[index, part],
            recv_sem=recv_sem.at[index, part],
            device_id={"seq": other},
            device_id_type=MESH,
        )

    def to_right(source, index, part):
        return carry_to(me + 1, right_sem, source, index, part)

    def to_left(source, index, part):
        return carry_to(me - 1, left_sem, source, index, part)

    for part in range(2):
        half = tok_ref.at[pl.ds(part * piece, piece)]

        @pl.when(has_right)
        def _(half=half, part=part):
            to_right(half, me, part).start()

        @pl.when(has_left)
        def _(half=half, part=part):
            to_left(half, me, part).start()

    bands = [(b, min(width, w2_hbm.shape[0] - b)) for b in range(0, w2_hbm.shape[0], width)]

    def load_band(i):
        begin, size = bands[i]
        return pltpu.make_async_copy(
            w2_hbm.at[pl.ds(begin, size)],
            win.at[pl.ds(0, size), pl.ds(begin, width)],
            w_sem.at[3 + i],
        )

    def order(n):
        step = (n + 1) // 2
        near = jnp.where(n % 2 == 1, me - step, me + step)
        far = jnp.where(2 * me < ranks, me + (n - short), me - (n - short))
        return jnp.where(n <= 2 * short, near, far)

    ids_row = ids_row_ref[...].astype(jnp.float32)
    chosen_row = (
        lax.broadcasted_iota(jnp.int32, (experts, rows), 0).astype(jnp.float32) == ids_row
    ).astype(jnp.float32)
    down = lax.broadcasted_iota(jnp.int32, (rows, rows), 0)
    across = lax.broadcasted_iota(jnp.int32, (rows, rows), 1)
    above = (down < across).astype(jnp.float32).astype(jnp.bfloat16)
    earlier_row = jnp.dot(chosen_row.astype(jnp.bfloat16), above, preferred_element_type=jnp.float32)
    slot_row = ids_row * most + jnp.sum(earlier_row * chosen_row, 0, keepdims=True)
    slot_column = jnp.sum(jnp.where(down == across, slot_row, 0.0), 1, keepdims=True)
    slot_rows[me] = jnp.broadcast_to(slot_row, slot_rows.shape[1:])

    def send_slots(other):
        return pltpu.make_async_remote_copy(
            src_ref=slot_rows.at[me],
            dst_ref=slot_rows.at[me],
            send_sem=slot_send.at[other],
            recv_sem=slot_recv.at[me],
            device_id=place(group, other),
            device_id_type=MESH,
        )

    def receive_slots(other):
        return pltpu.make_async_remote_copy(
            src_ref=slot_rows.at[other],
            dst_ref=slot_rows.at[other],
            send_sem=slot_send.at[other],
            recv_sem=slot_recv.at[other],
            device_id=place(group, other),
            device_id_type=MESH,
        )

    def start_slots(offset, carry):
        send_slots((me + offset) % ranks).start()
        return carry

    lax.fori_loop(1, ranks, start_slots, 0)

    def label(rank, shape, dim):
        column = lax.broadcasted_iota(jnp.int32, shape, dim).astype(jnp.float32)
        block = jnp.floor((column + 0.5) * (1.0 / most))
        return (block * ranks + rank.astype(jnp.float32)) * most + (column - block * most)

    shards[me, 0] = tok_ref[0:piece]
    shards[me, 1] = tok_ref[piece:rows]
    lane = lax.broadcasted_iota(jnp.int32, (slots, pair), 1)
    first = lane < head_dim
    own_label = label(me, (slots, rows), 0)
    col_block = 256 if width % 256 == 0 else width

    def project(pos, index, part):
        normed = normalize(shards[index, part].astype(jnp.float32), gain_ref[...]).astype(jnp.bfloat16)
        for c in range(0, 2 * width, col_block):
            kv[2 * pos + part, :, c : c + col_block] = jnp.dot(
                normed,
                win[:, width + c : width + c + col_block],
                preferred_element_type=jnp.float32,
            ).astype(jnp.bfloat16)

    def queries(pos, index):
        pick = (own_label == slot_rows[index, 0:1]).astype(jnp.float32).astype(jnp.bfloat16)
        chosen = jnp.dot(
            pick, shards[index].reshape(rows, width), preferred_element_type=jnp.float32
        )
        slot_tok[pos] = chosen.astype(jnp.bfloat16)
        project_queries(pos, chosen)

    def own_queries(e):
        project_queries(ranks + e, tok_ref[e * slots : (e + 1) * slots].astype(jnp.float32))

    def project_queries(pos, chosen):
        normed = normalize(chosen, gain_ref[...]).astype(jnp.bfloat16)
        for c in range(0, width, col_block):
            query[pos, :, c : c + col_block] = jnp.dot(
                normed, win[:, c : c + col_block], preferred_element_type=jnp.float32
            ).astype(jnp.bfloat16) * jnp.bfloat16(head_dim ** (-0.5))

    def scores_of(n, p, begin, end):
        keys = kv[begin:end, :, p * pair : (p + 1) * pair].reshape((end - begin) * piece, pair)
        both = query[n, :, p * pair : (p + 1) * pair]
        none = jnp.zeros_like(both)
        heads = jnp.concatenate([jnp.where(first, both, none), jnp.where(first, none, both)], 0)
        return lax.dot_general(
            heads, keys, (((1,), (1,)), ((), ())), preferred_element_type=jnp.float32
        )

    def mix(weights, p, begin, end):
        values = kv[begin:end, :, width + p * pair : width + (p + 1) * pair]
        values = values.reshape((end - begin) * piece, pair)
        return jnp.dot(
            weights,
            jnp.concatenate([values, jnp.ones_like(values)], 1),
            preferred_element_type=jnp.float32,
        )

    known = 2 * (ranks - 1)

    def kept(n):
        return jnp.where(n < ranks, n, n - 1)

    def begin_attention(n):
        a = kept(n)
        for p in range(pairs):
            scores = scores_of(n, p, 0, known)
            new = jnp.max(scores, -1, keepdims=True)
            update = mix(jnp.exp(scores - new).astype(jnp.bfloat16), p, 0, known)
            weight = update[:, pair : 2 * pair]
            acc[a, p] = update[:, 0:pair] / weight
            peak[a, :, p : p + 1] = new + jnp.log(weight[:, 0:1])

    def put_context(n, p, value, weight):
        mean = value / weight
        query[n, :, p * pair : (p + 1) * pair] = jnp.where(
            first, mean[0:slots], mean[slots : 2 * slots]
        ).astype(jnp.bfloat16)

    def end_attention(n):
        a = kept(n)
        for p in range(pairs):
            scores = scores_of(n, p, known, known + 2)
            old = jnp.broadcast_to(peak[a, :, p : p + 1], (2 * slots, pair))
            new = jnp.maximum(old, jnp.max(scores, -1, keepdims=True))
            scale = jnp.exp(old - new)
            spread = jnp.concatenate([new] * (rows // pair), 1) if rows % pair == 0 else new[:, 0:1]
            update = mix(jnp.exp(scores - spread).astype(jnp.bfloat16), p, known, known + 2)
            put_context(
                n,
                p,
                acc[a, p] * scale + update[:, 0:pair],
                scale + update[:, pair : 2 * pair],
            )

    def whole_attention(n):
        for p in range(pairs):
            scores = scores_of(n, p, 0, known + 2)
            new = jnp.max(scores, -1, keepdims=True)
            update = mix(jnp.exp(scores - new).astype(jnp.bfloat16), p, 0, known + 2)
            put_context(n, p, update[:, 0:pair], update[:, pair : 2 * pair])

    def over_plane(act):
        def one(offset, carry):
            act((group + offset) % groups)
            return carry

        lax.fori_loop(1, groups, one, 0)

    def send(n, other):
        return pltpu.make_async_remote_copy(
            src_ref=rows_buf.at[n, other],
            dst_ref=arrived.at[n, group],
            send_sem=out_sem.at[n, other],
            recv_sem=in_sem.at[n, group],
            device_id=place(other, me),
            device_id_type=MESH,
        )

    def receive(n, other):
        return pltpu.make_async_remote_copy(
            src_ref=rows_buf.at[n, other],
            dst_ref=arrived.at[n, other],
            send_sem=out_sem.at[n, other],
            recv_sem=in_sem.at[n, other],
            device_id=place(other, me),
            device_id_type=MESH,
        )

    def reply(n, other):
        return pltpu.make_async_remote_copy(
            src_ref=result.at[n, other],
            dst_ref=back.at[me, group],
            send_sem=reply_sem.at[n, other],
            recv_sem=back_sem.at[me, group],
            device_id=place(other, order(n)),
            device_id_type=MESH,
        )

    def returned(n, other):
        return pltpu.make_async_remote_copy(
            src_ref=result.at[n, other],
            dst_ref=back.at[order(n), other],
            send_sem=reply_sem.at[n, other],
            recv_sem=back_sem.at[order(n), other],
            device_id=place(other, order(n)),
            device_id_type=MESH,
        )

    def over_homes(n, act):
        def one(offset, carry):
            @pl.when((n > 0) | (offset > 0))
            def _():
                act((group + offset) % groups)

            return carry

        lax.fori_loop(0, groups, one, 0)

    def dispatch(n):
        rows_out = slot_tok[n].astype(jnp.float32) + jnp.dot(
            query[n], wout[...], preferred_element_type=jnp.float32
        )
        rows_buf[n] = (
            normalize(rows_out, gain2_ref[...]).astype(jnp.bfloat16).reshape(groups, most, width)
        )
        over_plane(lambda g: send(n, g).start())
        arrived[n, group] = rows_buf[n, group]

    hidden_units = w1.shape[1]
    block = 256 if hidden_units % 256 == 0 else hidden_units

    def work(n):
        over_plane(lambda g: receive(n, g).wait_recv())
        batch = arrived[n].reshape(slots, width)
        for c in range(0, hidden_units, block):
            inner[:, c : c + block] = jax.nn.relu(
                jnp.dot(batch, w1[:, c : c + block], preferred_element_type=jnp.float32)
            ).astype(jnp.bfloat16)
        for c in range(0, width, col_block):
            result[n, :, :, c : c + col_block] = (
                sum(
                    jnp.dot(
                        inner[:, b : b + size],
                        win[0:size, b + c : b + c + col_block],
                        preferred_element_type=jnp.float32,
                    )
                    for b, size in bands
                )
                .astype(jnp.bfloat16)
                .reshape(groups, most, col_block)
            )
        over_homes(n, lambda g: reply(n, g).start())

        @pl.when(n == 0)
        def _():
            back[me, group] = result[0, group]

    def finish_own(e):
        end_attention(ranks + e)
        begin_row = pl.multiple_of(e * slots, slots)
        own = pl.ds(begin_row, slots)
        rows_out = tok_ref[own].astype(jnp.float32) + jnp.dot(
            query[ranks + e], wout[...], preferred_element_type=jnp.float32
        )
        hidden[own] = rows_out
        gate[own] = lax.dot_general(
            normalize(rows_out, gain2_ref[...]).astype(jnp.bfloat16),
            router_ref[...],
            (((1,), (1,)), ((), ())),
            preferred_element_type=jnp.float32,
        )

    load_in.wait()
    project(0, me, 0)
    project(0, me, 1)
    queries(0, me)
    for e in range(extra):
        own_queries(e)

    def begin(n, carry):
        begin_attention(n)
        return carry

    def step(turn, carry):
        distance, part = 1 + turn // 2, turn % 2
        low, high = me - distance, me + distance

        @pl.when((distance == longest) & (part == 0))
        def _():
            lax.fori_loop(0, ranks - 1, begin, 0)
            lax.fori_loop(ranks, ranks + extra, begin, 0)

        @pl.when(low >= 0)
        def _():
            to_left(shards.at[low, part], low, part).wait_recv()

            @pl.when(has_right)
            def _():
                to_right(shards.at[low, part], low, part).start()

        @pl.when(high < ranks)
        def _():
            to_right(shards.at[high, part], high, part).wait_recv()

            @pl.when(has_left)
            def _():
                to_left(shards.at[high, part], high, part).start()

        def side(which, inner_carry):
            index = jnp.where(which == 0, low, high)
            pos = jnp.where(distance <= short, 2 * distance - 1 + which, short + distance)

            @pl.when((index >= 0) & (index < ranks))
            def _():
                project(pos, index, part)

                @pl.when((part == 1) & (distance < longest))
                def _():
                    receive_slots(index).wait_recv()
                    queries(pos, index)

            return inner_carry

        lax.fori_loop(0, 2, side, 0)
        return carry

    lax.fori_loop(0, 2 * (ranks - 1), step, 0)
    load_out.wait()
    end_attention(ranks - 2)
    dispatch(ranks - 2)
    receive_slots(order(ranks - 1)).wait_recv()
    queries(ranks - 1, order(ranks - 1))
    for i in range(len(bands)):
        load_band(i).start()
    whole_attention(ranks - 1)
    dispatch(ranks - 1)

    load1.wait()
    for i in range(len(bands)):
        load_band(i).wait()

    def chunk(turn):
        return jnp.where(turn == 0, ranks - 2, jnp.where(turn == 1, ranks - 1, ranks - 1 - turn))

    def experts_turn(turn, carry):
        @pl.when(turn + 2 < ranks)
        def _():
            end_attention(chunk(turn + 2))
            dispatch(chunk(turn + 2))

        own = turn + 2 - ranks

        @pl.when((own >= 0) & (own < extra))
        def _():
            finish_own(own)

        work(chunk(turn))
        return carry

    lax.fori_loop(0, ranks, experts_turn, 0)

    def own_turn(e, carry):
        finish_own(e)
        return carry

    lax.fori_loop(min(2, extra), extra, own_turn, 0)

    def arrival(n, carry):
        over_homes(n, lambda g: returned(n, g).wait_recv())
        return carry

    lax.fori_loop(0, ranks, arrival, 0)
    spot = lax.broadcasted_iota(jnp.int32, (rows, ranks * slots), 1).astype(jnp.float32)
    source = jnp.floor((spot + 0.5) * (1.0 / slots))
    spot = spot - source * slots
    target = jnp.floor((spot + 0.5) * (1.0 / most))
    spot = (target * ranks + source) * most + (spot - target * most)
    pick = (spot == slot_column).astype(jnp.float32).astype(jnp.bfloat16)
    own_expert = jnp.floor((slot_column + 0.5) * (1.0 / most))
    chosen = lax.broadcasted_iota(jnp.int32, (rows, experts), 1).astype(jnp.float32) == own_expert
    weight = jax.nn.sigmoid(jnp.sum(jnp.where(chosen, gate[...], 0.0), 1, keepdims=True))
    for c in range(0, width, col_block):
        combined = jnp.dot(
            pick,
            back[:, :, :, c : c + col_block].reshape(ranks * slots, col_block),
            preferred_element_type=jnp.float32,
        )
        out_ref[:, c : c + col_block] = (
            hidden[:, c : c + col_block] + weight * combined
        ).astype(jnp.bfloat16)

    def drain_rank(n, carry):
        over_plane(lambda g: send(n, g).wait_send())
        over_homes(n, lambda g: reply(n, g).wait_send())
        return carry

    lax.fori_loop(0, ranks, drain_rank, 0)

    def drain_slots(n, carry):
        send_slots((me + n) % ranks).wait_send()
        return carry

    lax.fori_loop(1, ranks, drain_slots, 0)

    def drain(index, carry):
        @pl.when(has_right & (index <= me))
        def _():
            for part in range(2):
                to_right(shards.at[index, part], index, part).wait_send()

        @pl.when(has_left & (index >= me))
        def _():
            for part in range(2):
                to_left(shards.at[index, part], index, part).wait_send()

        return carry

    lax.fori_loop(0, ranks, drain, 0)


def layer(tokens, expert_ids, attn_in, attn_out, gain_attn, gain_expert, router, w1, w2):
    rows, width = tokens.shape
    sizes = tuple(lax.axis_size(name) for name in AXES)
    groups, ranks = sizes[0] * sizes[1], sizes[2]
    devices = groups * ranks
    most = max(2, 2 * rows // devices)
    slots = groups * most
    head_dim = width // HEADS
    pair = 2 * head_dim
    pairs = width // pair
    vmem = pl.BlockSpec(memory_space=pltpu.VMEM)
    hbm = pl.BlockSpec(memory_space=pl.ANY)
    blocks = pltpu.VMEM((ranks, groups, most, width), jnp.bfloat16)
    extra = rows // slots
    per_rank = pltpu.SemaphoreType.DMA((ranks,))
    per_half = pltpu.SemaphoreType.DMA((ranks, 2))
    per_device = pltpu.SemaphoreType.DMA((ranks, groups))
    return pl.pallas_call(
        functools.partial(layer_kernel, sizes, head_dim),
        out_shape=jax.ShapeDtypeStruct((rows, width), jnp.bfloat16),
        in_specs=[vmem, vmem, hbm, hbm, vmem, vmem, vmem, hbm, hbm],
        out_specs=vmem,
        scratch_shapes=[
            pltpu.VMEM((ranks, 2, rows // 2, width), jnp.bfloat16),
            pltpu.VMEM((ranks, 8, rows), jnp.float32),
            pltpu.VMEM(attn_in.shape, jnp.bfloat16),
            pltpu.VMEM(attn_out.shape, jnp.bfloat16),
            pltpu.VMEM((ranks + extra, slots, width), jnp.bfloat16),
            pltpu.VMEM((2 * ranks, rows // 2, 2 * width), jnp.bfloat16),
            pltpu.VMEM((ranks - 1 + extra, pairs, 2 * slots, pair), jnp.float32),
            pltpu.VMEM((ranks - 1 + extra, 2 * slots, pairs), jnp.float32),
            pltpu.VMEM((ranks, slots, width), jnp.bfloat16),
            pltpu.VMEM((rows, width), jnp.float32),
            pltpu.VMEM((rows, devices), jnp.float32),
            blocks,
            blocks,
            blocks,
            blocks,
            pltpu.VMEM((slots, w1.shape[1]), jnp.bfloat16),
            pltpu.VMEM(w1.shape, jnp.bfloat16),
            pltpu.SemaphoreType.DMA((3 + -(-w2.shape[0] // width),)),
            per_half,
            per_half,
            per_half,
            per_rank,
            per_rank,
            per_device,
            per_device,
            per_device,
            per_device,
        ],
        compiler_params=pltpu.CompilerParams(
            collective_id=0, has_side_effects=True, vmem_limit_bytes=VMEM_LIMIT
        ),
    )(
        tokens,
        expert_ids.reshape(1, rows),
        attn_in,
        attn_out,
        gain_attn[None, :],
        gain_expert[None, :],
        router.T,
        w1,
        w2,
    )


def body(
    tokens, expert_ids, attn_in, attn_out, gain_attn, gain_expert, router, expert_in, expert_out
):
    return layer(
        tokens,
        expert_ids,
        attn_in,
        attn_out,
        gain_attn,
        gain_expert,
        router,
        expert_in[0],
        expert_out[0],
    )


def solution(mesh):
    return jax.shard_map(
        body,
        mesh=mesh,
        in_specs=(P(AXES, None), P(AXES, None), P(), P(), P(), P(), P(), P(AXES, None, None), P(AXES, None, None)),
        out_specs=P(AXES, None),
        check_vma=False,
    )
```

```python
import functools

import jax
import jax.numpy as jnp
from jax import lax
from jax.experimental import pallas as pl
from jax.experimental.pallas import tpu as pltpu
from jax.sharding import PartitionSpec as P

HEADS = 16
AXES = ("sec", "grp", "seq")
MESH = pl.DeviceIdType.MESH
VMEM_LIMIT = 60 * 1024 * 1024


def normalize(values, gain):
    return values * lax.rsqrt(jnp.mean(values * values, -1, keepdims=True) + 1e-06) * gain


def layer_kernel(
    sizes,
    head_dim,
    tok_ref,
    ids_row_ref,
    win_hbm,
    wout_hbm,
    gain_ref,
    gain2_ref,
    router_ref,
    w1_hbm,
    w2_hbm,
    out_ref,
    shards,
    slot_rows,
    win,
    wout,
    query,
    kv,
    acc,
    peak,
    slot_tok,
    hidden,
    gate,
    rows_buf,
    arrived,
    result,
    back,
    inner,
    w1,
    w_sem,
    right_sem,
    left_sem,
    recv_sem,
    slot_send,
    slot_recv,
    out_sem,
    in_sem,
    reply_sem,
    back_sem,
):
    secs, grps, ranks = sizes
    groups = secs * grps
    experts = groups * ranks
    most = rows_buf.shape[2]
    slots = groups * most
    rows, width = tok_ref.shape
    extra = rows // slots
    pair = 2 * head_dim
    pairs = width // pair
    piece = rows // 2
    me = lax.axis_index("seq")
    load_in = pltpu.make_async_copy(win_hbm, win, w_sem.at[0])
    load_out = pltpu.make_async_copy(wout_hbm, wout, w_sem.at[1])
    load1 = pltpu.make_async_copy(w1_hbm, w1, w_sem.at[2])
    load_in.start()
    load_out.start()
    load1.start()
    sec, grp = lax.axis_index("sec"), lax.axis_index("grp")
    group = sec * grps + grp
    has_left, has_right = me > 0, me < ranks - 1
    short = jnp.minimum(me, ranks - 1 - me)
    longest = ranks - 1 - short
    barrier = pltpu.get_barrier_semaphore()

    def place(other_group, other_rank):
        return (other_group // grps, other_group % grps, other_rank)

    def greet_column(offset, carry):
        pl.semaphore_signal(
            barrier, inc=1, device_id=place(group, (me + offset) % ranks), device_id_type=MESH
        )
        return carry

    def greet_plane(offset, carry):
        pl.semaphore_signal(
            barrier, inc=1, device_id=place((group + offset) % groups, me), device_id_type=MESH
        )
        return carry

    lax.fori_loop(1, ranks, greet_column, 0)
    lax.fori_loop(1, groups, greet_plane, 0)
    pl.semaphore_wait(barrier, ranks + groups - 2)

    def carry_to(other, sems, source, index, part):
        return pltpu.make_async_remote_copy(
            src_ref=source,
            dst_ref=shards.at[index, part],
            send_sem=sems.at[index, part],
            recv_sem=recv_sem.at[index, part],
            device_id={"seq": other},
            device_id_type=MESH,
        )

    def to_right(source, index, part):
        return carry_to(me + 1, right_sem, source, index, part)

    def to_left(source, index, part):
        return carry_to(me - 1, left_sem, source, index, part)

    for part in range(2):
        half = tok_ref.at[pl.ds(part * piece, piece)]

        @pl.when(has_right)
        def _(half=half, part=part):
            to_right(half, me, part).start()

        @pl.when(has_left)
        def _(half=half, part=part):
            to_left(half, me, part).start()

    bands = [(b, min(width, w2_hbm.shape[0] - b)) for b in range(0, w2_hbm.shape[0], width)]

    def load_band(i):
        begin, size = bands[i]
        return pltpu.make_async_copy(
            w2_hbm.at[pl.ds(begin, size)],
            win.at[pl.ds(0, size), pl.ds(begin, width)],
            w_sem.at[3 + i],
        )

    def order(n):
        step = (n + 1) // 2
        near = jnp.where(n % 2 == 1, me - step, me + step)
        far = jnp.where(2 * me < ranks, me + (n - short), me - (n - short))
        return jnp.where(n <= 2 * short, near, far)

    ids_row = ids_row_ref[...].astype(jnp.float32)
    chosen_row = (
        lax.broadcasted_iota(jnp.int32, (experts, rows), 0).astype(jnp.float32) == ids_row
    ).astype(jnp.float32)
    down = lax.broadcasted_iota(jnp.int32, (rows, rows), 0)
    across = lax.broadcasted_iota(jnp.int32, (rows, rows), 1)
    above = (down < across).astype(jnp.float32).astype(jnp.bfloat16)
    earlier_row = jnp.dot(chosen_row.astype(jnp.bfloat16), above, preferred_element_type=jnp.float32)
    slot_row = ids_row * most + jnp.sum(earlier_row * chosen_row, 0, keepdims=True)
    slot_column = jnp.sum(jnp.where(down == across, slot_row, 0.0), 1, keepdims=True)
    slot_rows[me] = jnp.broadcast_to(slot_row, slot_rows.shape[1:])

    def send_slots(other):
        return pltpu.make_async_remote_copy(
            src_ref=slot_rows.at[me],
            dst_ref=slot_rows.at[me],
            send_sem=slot_send.at[other],
            recv_sem=slot_recv.at[me],
            device_id=place(group, other),
            device_id_type=MESH,
        )

    def receive_slots(other):
        return pltpu.make_async_remote_copy(
            src_ref=slot_rows.at[other],
            dst_ref=slot_rows.at[other],
            send_sem=slot_send.at[other],
            recv_sem=slot_recv.at[other],
            device_id=place(group, other),
            device_id_type=MESH,
        )

    def start_slots(offset, carry):
        send_slots((me + offset) % ranks).start()
        return carry

    lax.fori_loop(1, ranks, start_slots, 0)

    def label(rank, shape, dim):
        column = lax.broadcasted_iota(jnp.int32, shape, dim).astype(jnp.float32)
        block = jnp.floor((column + 0.5) * (1.0 / most))
        return (block * ranks + rank.astype(jnp.float32)) * most + (column - block * most)

    shards[me, 0] = tok_ref[0:piece]
    shards[me, 1] = tok_ref[piece:rows]
    lane = lax.broadcasted_iota(jnp.int32, (slots, pair), 1)
    first = lane < head_dim
    own_label = label(me, (slots, rows), 0)
    col_block = 256 if width % 256 == 0 else width

    def project(pos, index, part):
        normed = normalize(shards[index, part].astype(jnp.float32), gain_ref[...]).astype(jnp.bfloat16)
        for c in range(0, 2 * width, col_block):
            kv[2 * pos + part, :, c : c + col_block] = jnp.dot(
                normed,
                win[:, width + c : width + c + col_block],
                preferred_element_type=jnp.float32,
            ).astype(jnp.bfloat16)

    def queries(pos, index):
        pick = (own_label == slot_rows[index, 0:1]).astype(jnp.float32).astype(jnp.bfloat16)
        chosen = jnp.dot(
            pick, shards[index].reshape(rows, width), preferred_element_type=jnp.float32
        )
        slot_tok[pos] = chosen.astype(jnp.bfloat16)
        project_queries(pos, chosen)

    def own_queries(e):
        project_queries(ranks + e, tok_ref[e * slots : (e + 1) * slots].astype(jnp.float32))

    def project_queries(pos, chosen):
        normed = normalize(chosen, gain_ref[...]).astype(jnp.bfloat16)
        for c in range(0, width, col_block):
            query[pos, :, c : c + col_block] = jnp.dot(
                normed, win[:, c : c + col_block], preferred_element_type=jnp.float32
            ).astype(jnp.bfloat16) * jnp.bfloat16(head_dim ** (-0.5))

    def scores_of(n, p, begin, end):
        keys = kv[begin:end, :, p * pair : (p + 1) * pair].reshape((end - begin) * piece, pair)
        both = query[n, :, p * pair : (p + 1) * pair]
        none = jnp.zeros_like(both)
        heads = jnp.concatenate([jnp.where(first, both, none), jnp.where(first, none, both)], 0)
        return lax.dot_general(
            heads, keys, (((1,), (1,)), ((), ())), preferred_element_type=jnp.float32
        )

    def mix(weights, p, begin, end):
        values = kv[begin:end, :, width + p * pair : width + (p + 1) * pair]
        values = values.reshape((end - begin) * piece, pair)
        return jnp.dot(
            weights,
            jnp.concatenate([values, jnp.ones_like(values)], 1),
            preferred_element_type=jnp.float32,
        )

    known = 2 * (ranks - 1)

    def begin_attention(n):
        ahead = scores_of(n, 0, 0, known)
        for p in range(pairs):
            scores = ahead
            if p + 1 < pairs:
                ahead = scores_of(n, p + 1, 0, known)
            new = jnp.max(scores, -1, keepdims=True)
            update = mix(jnp.exp(scores - new).astype(jnp.bfloat16), p, 0, known)
            weight = update[:, pair : 2 * pair]
            acc[n, p] = update[:, 0:pair] / weight
            peak[n, :, p : p + 1] = new + jnp.log(weight[:, 0:1])

    def put_context(n, p, value, weight):
        mean = value / weight
        query[n, :, p * pair : (p + 1) * pair] = jnp.where(
            first, mean[0:slots], mean[slots : 2 * slots]
        ).astype(jnp.bfloat16)

    def end_attention(n):
        ahead = scores_of(n, 0, known, known + 2)
        for p in range(pairs):
            scores = ahead
            if p + 1 < pairs:
                ahead = scores_of(n, p + 1, known, known + 2)
            old = jnp.broadcast_to(peak[n, :, p : p + 1], (2 * slots, pair))
            new = jnp.maximum(old, jnp.max(scores, -1, keepdims=True))
            scale = jnp.exp(old - new)
            spread = jnp.concatenate([new] * (rows // pair), 1) if rows % pair == 0 else new[:, 0:1]
            update = mix(jnp.exp(scores - spread).astype(jnp.bfloat16), p, known, known + 2)
            put_context(
                n,
                p,
                acc[n, p] * scale + update[:, 0:pair],
                scale + update[:, pair : 2 * pair],
            )

    def whole_attention(n):
        ahead = scores_of(n, 0, 0, known + 2)
        for p in range(pairs):
            scores = ahead
            if p + 1 < pairs:
                ahead = scores_of(n, p + 1, 0, known + 2)
            new = jnp.max(scores, -1, keepdims=True)
            update = mix(jnp.exp(scores - new).astype(jnp.bfloat16), p, 0, known + 2)
            put_context(n, p, update[:, 0:pair], update[:, pair : 2 * pair])

    def over_plane(act):
        def one(offset, carry):
            act((group + offset) % groups)
            return carry

        lax.fori_loop(1, groups, one, 0)

    def send(n, other):
        return pltpu.make_async_remote_copy(
            src_ref=rows_buf.at[n, other],
            dst_ref=arrived.at[n, group],
            send_sem=out_sem.at[n, other],
            recv_sem=in_sem.at[n, group],
            device_id=place(other, me),
            device_id_type=MESH,
        )

    def receive(n, other):
        return pltpu.make_async_remote_copy(
            src_ref=rows_buf.at[n, other],
            dst_ref=arrived.at[n, other],
            send_sem=out_sem.at[n, other],
            recv_sem=in_sem.at[n, other],
            device_id=place(other, me),
            device_id_type=MESH,
        )

    def reply(n, other):
        return pltpu.make_async_remote_copy(
            src_ref=result.at[n, other],
            dst_ref=back.at[me, group],
            send_sem=reply_sem.at[n, other],
            recv_sem=back_sem.at[me, group],
            device_id=place(other, order(n)),
            device_id_type=MESH,
        )

    def returned(n, other):
        return pltpu.make_async_remote_copy(
            src_ref=result.at[n, other],
            dst_ref=back.at[order(n), other],
            send_sem=reply_sem.at[n, other],
            recv_sem=back_sem.at[order(n), other],
            device_id=place(other, order(n)),
            device_id_type=MESH,
        )

    def over_homes(n, act):
        def one(offset, carry):
            @pl.when((n > 0) | (offset > 0))
            def _():
                act((group + offset) % groups)

            return carry

        lax.fori_loop(0, groups, one, 0)

    def dispatch(n):
        rows_out = slot_tok[n].astype(jnp.float32) + jnp.dot(
            query[n], wout[...], preferred_element_type=jnp.float32
        )
        rows_buf[n] = (
            normalize(rows_out, gain2_ref[...]).astype(jnp.bfloat16).reshape(groups, most, width)
        )
        over_plane(lambda g: send(n, g).start())
        arrived[n, group] = rows_buf[n, group]

    hidden_units = w1.shape[1]
    block = 256 if hidden_units % 256 == 0 else hidden_units

    def work(n):
        over_plane(lambda g: receive(n, g).wait_recv())
        batch = arrived[n].reshape(slots, width)
        for c in range(0, hidden_units, block):
            inner[:, c : c + block] = jax.nn.relu(
                jnp.dot(batch, w1[:, c : c + block], preferred_element_type=jnp.float32)
            ).astype(jnp.bfloat16)
        for c in range(0, width, col_block):
            result[n, :, :, c : c + col_block] = (
                sum(
                    jnp.dot(
                        inner[:, b : b + size],
                        win[0:size, b + c : b + c + col_block],
                        preferred_element_type=jnp.float32,
                    )
                    for b, size in bands
                )
                .astype(jnp.bfloat16)
                .reshape(groups, most, col_block)
            )
        over_homes(n, lambda g: reply(n, g).start())

        @pl.when(n == 0)
        def _():
            back[me, group] = result[0, group]

    def finish_own(e):
        whole_attention(ranks + e)
        begin_row = pl.multiple_of(e * slots, slots)
        own = pl.ds(begin_row, slots)
        rows_out = tok_ref[own].astype(jnp.float32) + jnp.dot(
            query[ranks + e], wout[...], preferred_element_type=jnp.float32
        )
        hidden[own] = rows_out
        gate[own] = lax.dot_general(
            normalize(rows_out, gain2_ref[...]).astype(jnp.bfloat16),
            router_ref[...],
            (((1,), (1,)), ((), ())),
            preferred_element_type=jnp.float32,
        )

    load_in.wait()
    project(0, me, 0)
    project(0, me, 1)
    queries(0, me)
    for e in range(extra):
        own_queries(e)

    def begin(n, carry):
        begin_attention(n)
        return carry

    def step(turn, carry):
        distance, part = 1 + turn // 2, turn % 2
        low, high = me - distance, me + distance

        @pl.when((distance == longest) & (part == 0))
        def _():
            lax.fori_loop(0, ranks - 1, begin, 0)

        @pl.when(low >= 0)
        def _():
            to_left(shards.at[low, part], low, part).wait_recv()

            @pl.when(has_right)
            def _():
                to_right(shards.at[low, part], low, part).start()

        @pl.when(high < ranks)
        def _():
            to_right(shards.at[high, part], high, part).wait_recv()

            @pl.when(has_left)
            def _():
                to_left(shards.at[high, part], high, part).start()

        def side(which, inner_carry):
            index = jnp.where(which == 0, low, high)
            pos = jnp.where(distance <= short, 2 * distance - 1 + which, short + distance)

            @pl.when((index >= 0) & (index < ranks))
            def _():
                project(pos, index, part)

                @pl.when((part == 1) & (distance < longest))
                def _():
                    receive_slots(index).wait_recv()
                    queries(pos, index)

            return inner_carry

        lax.fori_loop(0, 2, side, 0)
        return carry

    lax.fori_loop(0, 2 * (ranks - 1), step, 0)
    load_out.wait()
    end_attention(ranks - 2)
    dispatch(ranks - 2)
    receive_slots(order(ranks - 1)).wait_recv()
    queries(ranks - 1, order(ranks - 1))
    for i in range(len(bands)):
        load_band(i).start()
    whole_attention(ranks - 1)
    dispatch(ranks - 1)

    load1.wait()
    for i in range(len(bands)):
        load_band(i).wait()

    def chunk(turn):
        return jnp.where(turn == 0, ranks - 2, jnp.where(turn == 1, ranks - 1, ranks - 1 - turn))

    def experts_turn(turn, carry):
        @pl.when(turn + 2 < ranks)
        def _():
            end_attention(chunk(turn + 2))
            dispatch(chunk(turn + 2))

        work(chunk(turn))
        return carry

    lax.fori_loop(0, ranks, experts_turn, 0)

    def own_turn(e, carry):
        finish_own(e)
        return carry

    lax.fori_loop(0, extra, own_turn, 0)

    def arrival(n, carry):
        over_homes(n, lambda g: returned(n, g).wait_recv())
        return carry

    lax.fori_loop(0, ranks, arrival, 0)
    spot = lax.broadcasted_iota(jnp.int32, (rows, ranks * slots), 1).astype(jnp.float32)
    source = jnp.floor((spot + 0.5) * (1.0 / slots))
    spot = spot - source * slots
    target = jnp.floor((spot + 0.5) * (1.0 / most))
    spot = (target * ranks + source) * most + (spot - target * most)
    pick = (spot == slot_column).astype(jnp.float32).astype(jnp.bfloat16)
    own_expert = jnp.floor((slot_column + 0.5) * (1.0 / most))
    chosen = lax.broadcasted_iota(jnp.int32, (rows, experts), 1).astype(jnp.float32) == own_expert
    weight = jax.nn.sigmoid(jnp.sum(jnp.where(chosen, gate[...], 0.0), 1, keepdims=True))
    for c in range(0, width, col_block):
        combined = jnp.dot(
            pick,
            back[:, :, :, c : c + col_block].reshape(ranks * slots, col_block),
            preferred_element_type=jnp.float32,
        )
        out_ref[:, c : c + col_block] = (
            hidden[:, c : c + col_block] + weight * combined
        ).astype(jnp.bfloat16)

    def drain_rank(n, carry):
        over_plane(lambda g: send(n, g).wait_send())
        over_homes(n, lambda g: reply(n, g).wait_send())
        return carry

    lax.fori_loop(0, ranks, drain_rank, 0)

    def drain_slots(n, carry):
        send_slots((me + n) % ranks).wait_send()
        return carry

    lax.fori_loop(1, ranks, drain_slots, 0)

    def drain(index, carry):
        @pl.when(has_right & (index <= me))
        def _():
            for part in range(2):
                to_right(shards.at[index, part], index, part).wait_send()

        @pl.when(has_left & (index >= me))
        def _():
            for part in range(2):
                to_left(shards.at[index, part], index, part).wait_send()

        return carry

    lax.fori_loop(0, ranks, drain, 0)


def layer(tokens, expert_ids, attn_in, attn_out, gain_attn, gain_expert, router, w1, w2):
    rows, width = tokens.shape
    sizes = tuple(lax.axis_size(name) for name in AXES)
    groups, ranks = sizes[0] * sizes[1], sizes[2]
    devices = groups * ranks
    most = max(2, 2 * rows // devices)
    slots = groups * most
    head_dim = width // HEADS
    pair = 2 * head_dim
    pairs = width // pair
    vmem = pl.BlockSpec(memory_space=pltpu.VMEM)
    hbm = pl.BlockSpec(memory_space=pl.ANY)
    blocks = pltpu.VMEM((ranks, groups, most, width), jnp.bfloat16)
    extra = rows // slots
    per_rank = pltpu.SemaphoreType.DMA((ranks,))
    per_half = pltpu.SemaphoreType.DMA((ranks, 2))
    per_device = pltpu.SemaphoreType.DMA((ranks, groups))
    return pl.pallas_call(
        functools.partial(layer_kernel, sizes, head_dim),
        out_shape=jax.ShapeDtypeStruct((rows, width), jnp.bfloat16),
        in_specs=[vmem, vmem, hbm, hbm, vmem, vmem, vmem, hbm, hbm],
        out_specs=vmem,
        scratch_shapes=[
            pltpu.VMEM((ranks, 2, rows // 2, width), jnp.bfloat16),
            pltpu.VMEM((ranks, 8, rows), jnp.float32),
            pltpu.VMEM(attn_in.shape, jnp.bfloat16),
            pltpu.VMEM(attn_out.shape, jnp.bfloat16),
            pltpu.VMEM((ranks + extra, slots, width), jnp.bfloat16),
            pltpu.VMEM((2 * ranks, rows // 2, 2 * width), jnp.bfloat16),
            pltpu.VMEM((ranks - 1, pairs, 2 * slots, pair), jnp.float32),
            pltpu.VMEM((ranks - 1, 2 * slots, pairs), jnp.float32),
            pltpu.VMEM((ranks, slots, width), jnp.bfloat16),
            pltpu.VMEM((rows, width), jnp.float32),
            pltpu.VMEM((rows, devices), jnp.float32),
            blocks,
            blocks,
            blocks,
            blocks,
            pltpu.VMEM((slots, w1.shape[1]), jnp.bfloat16),
            pltpu.VMEM(w1.shape, jnp.bfloat16),
            pltpu.SemaphoreType.DMA((3 + -(-w2.shape[0] // width),)),
            per_half,
            per_half,
            per_half,
            per_rank,
            per_rank,
            per_device,
            per_device,
            per_device,
            per_device,
        ],
        compiler_params=pltpu.CompilerParams(
            collective_id=0, has_side_effects=True, vmem_limit_bytes=VMEM_LIMIT
        ),
    )(
        tokens,
        expert_ids.reshape(1, rows),
        attn_in,
        attn_out,
        gain_attn[None, :],
        gain_expert[None, :],
        router.T,
        w1,
        w2,
    )


def body(
    tokens, expert_ids, attn_in, attn_out, gain_attn, gain_expert, router, expert_in, expert_out
):
    return layer(
        tokens,
        expert_ids,
        attn_in,
        attn_out,
        gain_attn,
        gain_expert,
        router,
        expert_in[0],
        expert_out[0],
    )


def solution(mesh):
    return jax.shard_map(
        body,
        mesh=mesh,
        in_specs=(P(AXES, None), P(AXES, None), P(), P(), P(), P(), P(), P(AXES, None, None), P(AXES, None, None)),
        out_specs=P(AXES, None),
        check_vma=False,
    )
```
